32 devices in a mesh: section: 8 (over y, x, core), adapter: 4 (over z).
Axes of the slice: x: 2, y: 2, z: 4, core: 2. Of those that a mesh axis runs over, the one named last changes fastest.
Arguments:
- residual_input: bfloat16 [48, 4096], P(None, 'adapter'), may hold values from -6 to 6
- gains: float32 [8, 4096], P('section', 'adapter'), may hold values from 0.25 to 1.75
- frozen: bfloat16 [8, 4096, 4096], P('section', None, 'adapter'), may hold values from -0.046875 to 0.046875
- down_weight: bfloat16 [8, 4, 16, 4096], P('section', 'adapter'), may hold values from -0.09375 to 0.09375
- up_weight: bfloat16 [8, 4, 16, 4096], P('section', 'adapter'), may hold values from -1.5 to 1.5
- row_adapter_index: int32 [48, 1], replicated, may hold values from 0 to 3; in each aligned block of 12 rows (0 to 11, 12 to 23, ...) at most 4 rows name the same one
- head_output_cotangent: bfloat16 [8, 48, 4096], P('section', 'adapter'), may hold values from -6 to 6
Outputs:
- hidden_out: bfloat16 [8, 48, 4096], P('section', None, 'adapter')
- down_gradient: float32 [8, 4, 16, 4096], P('section', 'adapter')
- up_gradient: float32 [8, 4, 16, 4096], P('section', 'adapter')
The draws below stay inside these ranges and needn't reach their ends.
Inputs may be any that keep to these rules, and one draw needn't show every extreme that they name: `row_adapter_index`: in each aligned block of 12 rows (the rows of one index of adapter) no adapter is named by more than 4 rows.
All inputs are finite; a program needn't handle non-finite values.
Results may differ from the reference program's by a relative error of at most 0.0085.
Values may be sent and summed in bfloat16 or wider, within the bound.
A program may use at most 64 MiB of HBM per device.

```python
import math
import jax
import jax.numpy as jnp
import numpy as np
from jax import lax

RESIDUAL_WIDTH = 4096
ADAPTER_RANK = 16
CAP = 4
ROWS_DEV = 12
ADAPTER_COUNT = 4
ROWS = 48
FROZEN_LAYERS = 8


def steps_of(stream_key, dims, split, least, top_value):
    gain = 1.0
    for dim, shards_of in split:
        draws = jax.random.uniform(jax.random.fold_in(jax.random.fold_in(stream_key, 6), dim), (shards_of,), jnp.float32, least / len(split), top_value / len(split))
        gain = gain * jnp.repeat(jnp.exp(draws), dims[dim] // shards_of).reshape((-1,) + (1,) * (len(dims) - 1 - dim))
    return gain


def deal_out(key, own, number, rows, number_of, top, most, lean):
    ranking = jax.random.permutation(key, number_of)
    packed, ordinary = portions_of(number_of, rows * top, most, lean, True), portions_of(number_of, rows * top, most, lean, False)
    places = jnp.arange(number_of)

    def named(tallies, rotation):
        used = int((tallies > 0).sum())
        fixed = max(1, used // 4)
        moved = fixed + (places - fixed + rotation * (used - fixed)) % max(1, number_of - fixed)
        return jnp.zeros((number_of,), jnp.int32).at[ranking[jnp.where(places < fixed, places, moved)]].set(jnp.asarray(tallies, jnp.int32))

    tallies = jnp.where(number % 4 == 0, named(packed, number // 4), named(ordinary, number - number // 4 - 1))
    mixed = jax.random.permutation(jax.random.fold_in(own, 3), number_of)
    giver, receiver = mixed[0:number_of // 2 * 2:2], mixed[1:number_of // 2 * 2:2]
    room = jnp.minimum(tallies[giver] - 1, most - tallies[receiver]) // 2
    room = jnp.where((giver == ranking[0]) | (receiver == ranking[0]) | (tallies[receiver] == 0), 0, jnp.maximum(room, 0))
    moved = jax.random.randint(jax.random.fold_in(own, 4), (number_of // 2,), 0, 1 << 20) % (room + 1)
    tallies = tallies.at[giver].add(-moved).at[receiver].add(moved)
    items = jnp.searchsorted(jnp.cumsum(tallies), jnp.arange(rows * top), side="right").astype(jnp.int32)
    table = items.reshape(top, rows).T
    table = table[jax.random.permutation(jax.random.fold_in(own, 1), rows)]
    rotation = jax.random.randint(jax.random.fold_in(own, 2), (rows, 1), 0, top)
    return jnp.take_along_axis(table, (jnp.arange(top)[None, :] + rotation) % top, axis=1)


def portions_of(count, total, reach, skew, full):
    portions = [(1 << 20) // math.isqrt(grade ** skew) + 1 for grade in range(1, count + 1)]
    largest = reach if full else min(reach, max(-(-total // count), total * portions[0] // sum(portions)))
    least = 1 if total - largest >= count - 1 else 0
    given, spare = [largest] + [least] * (count - 1), total - largest - least * (count - 1)
    while spare > 0:
        movable = [i for i in range(1, count) if given[i] < largest] or [i for i in range(1, count) if given[i] < reach]
        whole, remaining = sum([portions[i] for i in movable]), spare
        for i in movable:
            addition = min(reach - given[i], max(1, remaining * portions[i] // whole), spare)
            given[i] = given[i] + addition
            spare = spare - addition
    return np.array(given)


def normal_values(key, extent, scale, most, split=(), dtype=jnp.bfloat16):
    values = scale * jax.random.normal(key, extent, jnp.float32)
    if split:
        values = values * steps_of(key, extent, split, -0.22, 0.18)
    return jnp.clip(values, -most, most).astype(dtype)


def setup_inputs(seed: int = 0) -> dict:
    keys = jax.random.split(jax.random.key(seed), 8)
    residual_input = normal_values(keys[0], (ROWS, RESIDUAL_WIDTH), 1.0, 6.0, ((1, 4),))
    gains = jnp.clip(1.0 + 0.15 * jax.random.normal(keys[1], (FROZEN_LAYERS, RESIDUAL_WIDTH), jnp.float32), 0.25, 1.75)
    frozen = normal_values(keys[2], (FROZEN_LAYERS, RESIDUAL_WIDTH, RESIDUAL_WIDTH), (4 * RESIDUAL_WIDTH) ** -0.5, 0.046875, ((0, 8), (2, 4)))
    down_weight = normal_values(keys[3], (FROZEN_LAYERS, ADAPTER_COUNT, ADAPTER_RANK, RESIDUAL_WIDTH), RESIDUAL_WIDTH ** -0.5, 0.09375, ((0, 8), (1, 4)))
    up_weight = normal_values(keys[4], (FROZEN_LAYERS, ADAPTER_COUNT, ADAPTER_RANK, RESIDUAL_WIDTH), ADAPTER_RANK ** -0.5, 1.5, ((0, 8), (1, 4)))
    row_adapter_index_keys = jax.random.split(jax.random.fold_in(keys[5], 1), ROWS // ROWS_DEV)
    row_adapter_index_turns = jax.random.permutation(jax.random.fold_in(keys[5], 3), ROWS // ROWS_DEV)
    row_adapter_index = jax.vmap(lambda own, number: deal_out(jax.random.fold_in(keys[5], 2), own, number, ROWS_DEV, ADAPTER_COUNT, 1, CAP, 2))(row_adapter_index_keys, row_adapter_index_turns).reshape((ROWS, 1))
    head_output_cotangent = normal_values(keys[6], (FROZEN_LAYERS, ROWS, RESIDUAL_WIDTH), 1.0, 6.0, ((0, 8), (1, 4)))
    return dict(residual_input=residual_input, gains=gains, frozen=frozen, down_weight=down_weight, up_weight=up_weight, row_adapter_index=row_adapter_index, head_output_cotangent=head_output_cotangent)


epsilon = 1e-05
adapter_scale = 2.0

def reference(residual_input, gains, frozen, down_weight, up_weight, row_adapter_index, head_output_cotangent):
    adapter_of = row_adapter_index[:, 0]
    hidden = residual_input
    hidden_list = []
    down_list = []
    up_list = []
    for layer_index in range(FROZEN_LAYERS):
        stream = hidden.astype(jnp.float32)
        mean_square = lax.optimization_barrier(jnp.mean(stream * stream, axis=1, keepdims=True))
        normed = (stream * lax.rsqrt(mean_square + epsilon) * gains[layer_index][None, :]).astype(jnp.bfloat16)
        hidden = (stream + jnp.dot(normed, frozen[layer_index], preferred_element_type=jnp.float32)).astype(jnp.bfloat16)
        hidden_list.append(hidden)
        cotangent = head_output_cotangent[layer_index]
        down_gradient_list = []
        up_gradient_list = []
        for adapter_number in range(ADAPTER_COUNT):
            belongs = (adapter_of == adapter_number)[:, None]
            normed_masked_rows = jnp.where(belongs, normed, jnp.zeros_like(normed))
            cotangent_masked = jnp.where(belongs, cotangent, jnp.zeros_like(cotangent))
            rank_projection = jnp.dot(normed_masked_rows, down_weight[layer_index, adapter_number].T, preferred_element_type=jnp.float32).astype(jnp.bfloat16)
            rank_cotangent = jnp.dot(cotangent_masked, up_weight[layer_index, adapter_number].T, preferred_element_type=jnp.float32).astype(jnp.bfloat16)
            up_gradient_list.append(adapter_scale * jnp.dot(rank_projection.T, cotangent_masked, preferred_element_type=jnp.float32))
            down_gradient_list.append(adapter_scale * jnp.dot(rank_cotangent.T, normed_masked_rows, preferred_element_type=jnp.float32))
        down_list.append(jnp.stack(down_gradient_list))
        up_list.append(jnp.stack(up_gradient_list))
    return (jnp.stack(hidden_list), jnp.stack(down_list), jnp.stack(up_list))
```

```python
import functools
import jax
import jax.numpy as jnp
from jax import lax
from jax.experimental import pallas as pl
from jax.experimental.pallas import tpu as pltpu
from jax.sharding import PartitionSpec as P

MICRO_ROWS = 8
DONOR = 2
CAP = 4
epsilon = 1e-05
adapter_scale = 2.0
MESH = pl.DeviceIdType.MESH
CONTRACT_LAST = (((1,), (1,)), ((), ()))


def as_bits(mask):
    return jnp.where(mask, 1.0, 0.0).astype(jnp.bfloat16)


def dot(a, b):
    return jnp.dot(a, b, preferred_element_type=jnp.float32)


def dot_t(a, b):
    return lax.dot_general(a, b, CONTRACT_LAST, preferred_element_type=jnp.float32)


def relay(
    S,
    A,
    x_ref,
    gain_ref,
    w_ref,
    down_ref,
    up_ref,
    idx_ref,
    cot_ref,
    hid_ref,
    dgrad_ref,
    ugrad_ref,
    w_buf,
    h_buf,
    x_buf,
    s_buf,
    g_buf,
    n_buf,
    inv_buf,
    c_buf,
    acc_buf,
    d_buf,
    u_buf,
    i_buf,
    r_buf,
    back_buf,
    pick_buf,
    p_buf,
    o_buf,
    q_buf,
    go_sem,
    in_sem,
    x_sem,
    w_sem,
    xs_sem,
    hs_sem,
    hr_sem,
    gs_sem,
    gr_sem,
    cs_sem,
    cr_sem,
):
    s = lax.axis_index("section")
    a = lax.axis_index("adapter")
    NM, _, MR, C = h_buf.shape
    rows = n_buf.shape[1]
    width = A * C
    RD = cot_ref.shape[1]
    RP = p_buf.shape[0]
    paired = A & (A - 1) == 0
    order = [0, *range(A // 2, A), *range(1, A // 2)]
    donor = DONOR

    def w_copy(j):
        part = pl.ds(pl.multiple_of(j * C, C), C)
        return pltpu.make_async_copy(w_ref.at[0, part], w_buf.at[part], w_sem.at[j])

    def peer(d):
        if not paired:
            return lax.rem(a + d, A)
        place, bit = 0, 1
        while bit < A:
            place = place + lax.rem(a // bit + (d // bit) % 2, 2) * bit
            bit *= 2
        return place

    def back_peer(d):
        return peer(d) if paired else lax.rem(a + A - d, A)

    barrier = pltpu.get_barrier_semaphore()

    def greet(section, j):
        pl.semaphore_signal(
            barrier, inc=1, device_id=(section, j), device_id_type=MESH
        )

    for d in range(A - 1, 0, -1):
        greet(s, peer(d))

    @pl.when(s > 0)
    def _():
        for d in range(A - 1, -1, -1):
            greet(s - 1, peer(d))

    @pl.when(s < S - 1)
    def _():
        for d in range(A - 1, -1, -1):
            greet(s + 1, peer(d))

    @pl.when(s == 0)
    def _():
        for d in range(A - 1, 0, -1):
            greet(donor, peer(d))

    g_load = pltpu.make_async_copy(gain_ref, g_buf.at[a], in_sem.at[0])
    c_load = pltpu.make_async_copy(cot_ref.at[0], r_buf, in_sem.at[1])
    d_load = pltpu.make_async_copy(down_ref.at[0, 0], d_buf, in_sem.at[2])
    u_load = pltpu.make_async_copy(up_ref.at[0, 0], u_buf, in_sem.at[3])
    i_load = pltpu.make_async_copy(idx_ref, i_buf, in_sem.at[4])

    def x_load(m):
        return pltpu.make_async_copy(
            x_ref.at[pl.ds(m * MR, MR)], h_buf.at[m, a], x_sem.at[m]
        )

    g_load.start()

    @pl.when(s == 0)
    def _():
        for m in range(NM):
            x_load(m).start()

    def x_fetch(m):
        return pltpu.make_async_copy(
            x_ref.at[pl.ds(m * MR, MR)], x_buf.at[m], x_sem.at[m]
        )

    @pl.when(s == donor)
    def _():
        for m in range(1, NM):
            x_fetch(m).start()

    for d in range(A):
        w_copy(peer(d)).start()
    for load in (c_load, d_load, u_load, i_load):
        load.start()

    def remote(src, dst, send, recv, section, j):
        return pltpu.make_async_remote_copy(
            src_ref=src,
            dst_ref=dst,
            send_sem=send,
            recv_sem=recv,
            device_id=(section, j),
            device_id_type=MESH,
        )

    def x_copy(m, j, block):
        return remote(
            h_buf.at[m, a],
            h_buf.at[m, block],
            xs_sem.at[m, j],
            hr_sem.at[m, block],
            s,
            j,
        )

    def y_copy(m, j, block):
        return remote(
            x_buf.at[m],
            h_buf.at[m, block],
            xs_sem.at[m, j],
            hr_sem.at[m, block],
            0,
            j,
        )

    def h_copy(m, j, block):
        return remote(
            s_buf.at[m], h_buf.at[m, block], hs_sem.at[m, j], hr_sem.at[m, block], s + 1, j
        )

    def g_copy(j, block):
        return remote(g_buf.at[a], g_buf.at[block], gs_sem.at[j], gr_sem.at[block], s, j)

    def c_copy(j, block):
        return remote(o_buf.at[j], c_buf.at[block], cs_sem.at[j], cr_sem.at[block], s, j)

    g_load.wait()

    @pl.when(s == 0)
    def _():
        for m in range(NM):
            x_load(m).wait()

    before = (s + S - 1) // S
    after = (2 * S - 2 - s) // S
    count = A - 1 + A * (before + after)
    pl.semaphore_wait(barrier, count + jnp.where(s == donor, A - 1, 0))

    @pl.when(s == 0)
    def _():
        for d in range(A - 1, 0, -1):
            x_copy(0, back_peer(d), a).start()
            g_copy(back_peer(d), a).start()

    @pl.when(s == donor)
    def _():
        for m in range(1, NM):
            x_fetch(m).wait()
            for d in range(A - 1, 0, -1):
                y_copy(m, back_peer(d), a).start()

    @pl.when(s > 0)
    def _():
        for d in range(A - 1, 0, -1):
            g_copy(back_peer(d), a).start()

    def send_rows():
        c_load.wait()
        i_load.wait()
        shape = (A * CAP, rows)
        slot = lax.broadcasted_iota(jnp.int32, shape, 0)
        row = lax.broadcasted_iota(jnp.int32, shape, 1)
        one = lax.broadcasted_iota(jnp.int32, (rows, rows), 0)
        two = lax.broadcasted_iota(jnp.int32, (rows, rows), 1)
        earlier = as_bits((one // RD == two // RD) & (one < two))
        theirs = i_buf[...] == slot // CAP
        rank = dot(as_bits(theirs), earlier)
        chosen = as_bits(theirs & (rank == (slot % CAP).astype(jnp.float32)))
        local = as_bits(
            (lax.broadcasted_iota(jnp.int32, (rows, RP), 0) - a * RD
             == lax.broadcasted_iota(jnp.int32, (rows, RP), 1))
            & (lax.broadcasted_iota(jnp.int32, (rows, RP), 1) < RD)
        )
        chosen = dot(chosen, local).astype(jnp.bfloat16)
        p_buf[...] = jnp.zeros((RP, width), jnp.bfloat16)
        p_buf[pl.ds(0, RD), :] = r_buf[...]
        packed = dot(chosen, p_buf[...])
        for j in range(A):
            o_buf[j] = packed[j * CAP : (j + 1) * CAP].astype(jnp.bfloat16)
        for d in range(1, A):
            c_copy(back_peer(d), a).start()
        c_buf[a] = o_buf[a]
        own = i_buf[...] == a
        own = own & (row >= 0)
        rank = dot(as_bits(own), earlier)
        mine = own & (row // RD == slot // CAP) & (rank == (slot % CAP).astype(jnp.float32))
        pick_buf[...] = as_bits(mine)

    def project_rows():
        u_load.wait()
        for d in range(1, A):
            c_copy(peer(d), peer(d)).wait_recv()
        for j in range(A):
            q_buf[j * CAP : (j + 1) * CAP, :] = c_buf[j].astype(jnp.float32)
        back = dot_t(u_buf[...], q_buf[...].astype(jnp.bfloat16)).astype(jnp.bfloat16)
        back_buf[...] = dot(back, pick_buf[...])

    @pl.when(s >= 2)
    def _():
        send_rows()

    for d in range(1, A):
        g_copy(peer(d), peer(d)).wait_recv()

    @pl.when(s >= 2)
    def _():
        project_rows()

    d_load.wait()
    for d in range(A):
        w_copy(peer(d)).wait()

    def micro(m, carry):
        start = pl.multiple_of(m * MR, MR)
        squares = jnp.zeros((MR, 128), jnp.float32)
        for d in range(A):
            j = peer(d)
            if d == 0:

                @pl.when(s > 0)
                def _():
                    h_copy(m, a, a).wait_recv()

            else:
                h_copy(m, a, j).wait_recv()
            h = h_buf[m, j].astype(jnp.float32)
            for t in range(C // 128):
                part = h[:, t * 128 : (t + 1) * 128]
                squares = squares + part * part
            h = h * g_buf[j]
            scaled = h.astype(jnp.bfloat16)
            n_buf[j, pl.ds(start, MR), :] = h
            part = dot(scaled, w_buf[pl.ds(pl.multiple_of(j * C, C), C), :])
            if d == 0:
                acc_buf[...] = part
            elif d < A - 1:
                acc_buf[...] += part
        inverse = lax.rsqrt(jnp.sum(squares, axis=1, keepdims=True) / width + epsilon)
        total = acc_buf[...] + part
        result = (h_buf[m, a].astype(jnp.float32) + total * inverse).astype(jnp.bfloat16)
        s_buf[m] = result

        @pl.when(s < S - 1)
        def _():
            for d in order:
                h_copy(m, back_peer(d), a).start()

        hid_ref[0, pl.ds(start, MR), :] = result
        inv_buf[pl.ds(start, MR), :] = jnp.broadcast_to(inverse, (MR, 128))
        return carry

    lax.fori_loop(0, NM, micro, 0)

    def release(section):
        pl.semaphore_signal(go_sem, inc=1, device_id=(section, a), device_id_type=MESH)

    @pl.when(s == 2)
    def _():
        release(1)

    @pl.when(s == 1)
    def _():
        pl.semaphore_wait(go_sem, 1)
        release(0)

    @pl.when(s == 0)
    def _():
        pl.semaphore_wait(go_sem, 1)

    @pl.when(s < 2)
    def _():
        send_rows()
        project_rows()

    eye = (lax.broadcasted_iota(jnp.int32, (rows, rows), 0)
           == lax.broadcasted_iota(jnp.int32, (rows, rows), 1))
    inverse = jnp.sum(jnp.where(eye, inv_buf[:, :1], 0.0), axis=0, keepdims=True)
    back = (back_buf[...] * inverse).astype(jnp.bfloat16)
    low = jnp.zeros(back.shape, jnp.float32)
    for j in range(A):
        block = n_buf[j].astype(jnp.bfloat16)
        low = low + dot_t(d_buf[:, j * C : (j + 1) * C], block)
        dgrad_ref[0, 0, :, j * C : (j + 1) * C] = adapter_scale * dot(back, block)
    low = (low * inverse).astype(jnp.bfloat16)
    low_mine = dot_t(low, pick_buf[...]).astype(jnp.bfloat16)
    ugrad_ref[0, 0] = adapter_scale * dot(low_mine, q_buf[...].astype(jnp.bfloat16))

    for d in range(1, A):
        g_copy(peer(d), a).wait_send()
        c_copy(peer(d), a).wait_send()

    @pl.when(s == 0)
    def _():
        for d in range(1, A):
            x_copy(0, peer(d), a).wait_send()

    @pl.when(s == donor)
    def _():
        for m in range(1, NM):
            for d in range(1, A):
                y_copy(m, peer(d), a).wait_send()

    @pl.when(s < S - 1)
    def _():
        for m in range(NM):
            for d in range(A):
                h_copy(m, peer(d), a).wait_send()


def store(*refs):
    copies = [
        pltpu.make_async_copy(refs[k], refs[3 + k], refs[6].at[k]) for k in range(3)
    ]
    for copy in copies:
        copy.start()
    for copy in copies:
        copy.wait()


def store(*refs):
    copies = [
        pltpu.make_async_copy(refs[k], refs[3 + k], refs[6].at[k]) for k in range(3)
    ]
    for copy in copies:
        copy.start()
    for copy in copies:
        copy.wait()


def body(S, A, x, gains, frozen, down, up, idx, cot):
    rows, C = x.shape
    width = C * A
    rank = down.shape[2]
    MR = MICRO_ROWS
    NM = rows // MR
    RP = -(-cot.shape[1] // 16) * 16
    args = (x, gains, frozen, down, up, idx.T, cot)
    vmem = pl.BlockSpec(memory_space=pltpu.VMEM)
    hbm = pl.BlockSpec(memory_space=pltpu.HBM)
    dma = pltpu.SemaphoreType.DMA
    shapes = (
        jax.ShapeDtypeStruct((1, rows, C), jnp.bfloat16),
        jax.ShapeDtypeStruct((1, 1, rank, width), jnp.float32),
        jax.ShapeDtypeStruct((1, 1, rank, width), jnp.float32),
    )
    results = pl.pallas_call(
        functools.partial(relay, S, A),
        out_shape=shapes,
        in_specs=[hbm] * 7,
        out_specs=(vmem, vmem, vmem),
        scratch_shapes=[
            pltpu.VMEM((width, C), jnp.bfloat16),
            pltpu.VMEM((NM, A, MR, C), jnp.bfloat16),
            pltpu.VMEM((NM, MR, C), jnp.bfloat16),
            pltpu.VMEM((NM, MR, C), jnp.bfloat16),
            pltpu.VMEM((A, 1, C), jnp.float32),
            pltpu.VMEM((A, rows, C), jnp.float32),
            pltpu.VMEM((rows, 128), jnp.float32),
            pltpu.VMEM((A, CAP, width), jnp.bfloat16),
            pltpu.VMEM((MR, C), jnp.float32),
            pltpu.VMEM((rank, width), jnp.bfloat16),
            pltpu.VMEM((rank, width), jnp.bfloat16),
            pltpu.VMEM((1, rows), jnp.int32),
            pltpu.VMEM((cot.shape[1], width), jnp.bfloat16),
            pltpu.VMEM((rank, rows), jnp.float32),
            pltpu.VMEM((A * CAP, rows), jnp.bfloat16),
            pltpu.VMEM((RP, width), jnp.bfloat16),
            pltpu.VMEM((A, CAP, width), jnp.bfloat16),
            pltpu.VMEM((A * CAP, width), jnp.float32),
            pltpu.SemaphoreType.REGULAR,
            dma((5,)),
            dma((NM,)),
            dma((A,)),
            dma((NM, A)),
            dma((NM, A)),
            dma((NM, A)),
            dma((A,)),
            dma((A,)),
            dma((A,)),
            dma((A,)),
        ],
        compiler_params=pltpu.CompilerParams(
            collective_id=0, has_side_effects=True, vmem_limit_bytes=48 * 1024 * 1024
        ),
        name="relay",
    )(*[pltpu.with_memory_space_constraint(v, pltpu.HBM) for v in args])
    return pl.pallas_call(
        store,
        out_shape=shapes,
        in_specs=[vmem] * 3,
        out_specs=(hbm, hbm, hbm),
        scratch_shapes=[dma((3,))],
        name="store",
    )(*[pltpu.with_memory_space_constraint(v, pltpu.VMEM) for v in results])


def solution(mesh):
    in_specs = (
        P(None, "adapter"),
        P("section", "adapter"),
        P("section", None, "adapter"),
        P("section", "adapter", None, None),
        P("section", "adapter", None, None),
        P(),
        P("section", "adapter", None),
    )
    out_specs = (
        P("section", None, "adapter"),
        P("section", "adapter", None, None),
        P("section", "adapter", None, None),
    )
    step = functools.partial(body, mesh.shape["section"], mesh.shape["adapter"])
    return jax.shard_map(step, mesh=mesh, in_specs=in_specs, out_specs=out_specs, check_vma=False)
```

```python
import functools
import jax
import jax.numpy as jnp
from jax import lax
from jax.experimental import pallas as pl
from jax.experimental.pallas import tpu as pltpu
from jax.sharding import PartitionSpec as P

MICRO_ROWS = 8
DONOR = 3
CAP = 4
epsilon = 1e-05
adapter_scale = 2.0
MESH = pl.DeviceIdType.MESH
CONTRACT_LAST = (((1,), (1,)), ((), ()))


def as_bits(mask):
    return jnp.where(mask, 1.0, 0.0).astype(jnp.bfloat16)


def dot(a, b):
    return jnp.dot(a, b, preferred_element_type=jnp.float32)


def dot_t(a, b):
    return lax.dot_general(a, b, CONTRACT_LAST, preferred_element_type=jnp.float32)


def relay(
    S,
    A,
    x_ref,
    gain_ref,
    w_ref,
    down_ref,
    up_ref,
    idx_ref,
    cot_ref,
    hid_ref,
    dgrad_ref,
    ugrad_ref,
    w_buf,
    h_buf,
    x_buf,
    s_buf,
    g_buf,
    n_buf,
    inv_buf,
    c_buf,
    acc_buf,
    d_buf,
    u_buf,
    i_buf,
    r_buf,
    back_buf,
    pick_buf,
    p_buf,
    o_buf,
    q_buf,
    go_sem,
    in_sem,
    x_sem,
    w_sem,
    xs_sem,
    hs_sem,
    hr_sem,
    gs_sem,
    gr_sem,
    cs_sem,
    cr_sem,
):
    s = lax.axis_index("section")
    a = lax.axis_index("adapter")
    NM, _, MR, C = h_buf.shape
    rows = n_buf.shape[1]
    width = A * C
    RD = cot_ref.shape[1]
    RP = p_buf.shape[0]
    paired = A & (A - 1) == 0
    order = [0, *range(A // 2, A), *range(1, A // 2)]
    donor = DONOR

    def w_copy(j):
        part = pl.ds(pl.multiple_of(j * C, C), C)
        return pltpu.make_async_copy(w_ref.at[0, part], w_buf.at[part], w_sem)

    def peer(d):
        if not paired:
            return lax.rem(a + d, A)
        place, bit = 0, 1
        while bit < A:
            place = place + lax.rem(a // bit + (d // bit) % 2, 2) * bit
            bit *= 2
        return place

    def back_peer(d):
        return peer(d) if paired else lax.rem(a + A - d, A)

    barrier = pltpu.get_barrier_semaphore()

    def greet(section, j):
        pl.semaphore_signal(
            barrier, inc=1, device_id=(section, j), device_id_type=MESH
        )

    for d in range(A - 1, 0, -1):
        greet(s, peer(d))

    @pl.when(s > 0)
    def _():
        for d in range(A - 1, -1, -1):
            greet(s - 1, peer(d))

    @pl.when(s < S - 1)
    def _():
        for d in range(A - 1, -1, -1):
            greet(s + 1, peer(d))

    @pl.when(s == 0)
    def _():
        for d in range(A - 1, 0, -1):
            greet(donor, peer(d))

    g_load = pltpu.make_async_copy(gain_ref, g_buf.at[a], in_sem.at[0])
    c_load = pltpu.make_async_copy(cot_ref.at[0], r_buf, in_sem.at[1])
    d_load = pltpu.make_async_copy(down_ref.at[0, 0], d_buf, in_sem.at[2])
    u_load = pltpu.make_async_copy(up_ref.at[0, 0], u_buf, in_sem.at[3])
    i_load = pltpu.make_async_copy(idx_ref, i_buf, in_sem.at[4])

    def x_load(m):
        return pltpu.make_async_copy(
            x_ref.at[pl.ds(m * MR, MR)], h_buf.at[m, a], x_sem
        )

    g_load.start()

    @pl.when(s == 0)
    def _():
        for m in range(NM):
            x_load(m).start()

    def x_fetch(m):
        return pltpu.make_async_copy(
            x_ref.at[pl.ds(m * MR, MR)], x_buf.at[m], x_sem
        )

    @pl.when(s == donor)
    def _():
        for m in range(1, NM):
            x_fetch(m).start()

    for d in range(A):
        w_copy(peer(d)).start()
    for load in (c_load, d_load, u_load, i_load):
        load.start()

    def remote(src, dst, send, recv, section, j):
        return pltpu.make_async_remote_copy(
            src_ref=src,
            dst_ref=dst,
            send_sem=send,
            recv_sem=recv,
            device_id=(section, j),
            device_id_type=MESH,
        )

    def x_copy(m, j, block):
        return remote(
            h_buf.at[m, a],
            h_buf.at[m, block],
            xs_sem,
            hr_sem.at[m, block],
            s,
            j,
        )

    def y_copy(m, j, block):
        return remote(
            x_buf.at[m],
            h_buf.at[m, block],
            xs_sem,
            hr_sem.at[m, block],
            0,
            j,
        )

    def h_copy(m, j, block):
        return remote(
            s_buf.at[m], h_buf.at[m, block], hs_sem, hr_sem.at[m, block], s + 1, j
        )

    def g_copy(j, block):
        return remote(g_buf.at[a], g_buf.at[block], gs_sem, gr_sem, s, j)

    def c_copy(j, block):
        return remote(o_buf.at[j], c_buf.at[block], cs_sem, cr_sem, s, j)

    g_others = g_buf.at[pl.ds(0, A - 1)]
    c_others = c_buf.at[pl.ds(0, A - 1)]
    g_load.wait()

    @pl.when(s == 0)
    def _():
        pltpu.make_async_copy(x_buf, h_buf.at[:, a], x_sem).wait()

    before = (s + S - 1) // S
    after = (2 * S - 2 - s) // S
    count = A - 1 + A * (before + after)
    pl.semaphore_wait(barrier, count + jnp.where(s == donor, A - 1, 0))

    @pl.when(s == 0)
    def _():
        for d in range(A - 1, 0, -1):
            x_copy(0, back_peer(d), a).start()
            g_copy(back_peer(d), a).start()

    @pl.when(s == donor)
    def _():
        late = x_buf.at[pl.ds(1, NM - 1)]
        pltpu.make_async_copy(late, late, x_sem).wait()
        for m in range(1, NM):
            for d in range(A - 1, 0, -1):
                y_copy(m, back_peer(d), a).start()

    @pl.when(s > 0)
    def _():
        for d in range(A - 1, 0, -1):
            g_copy(back_peer(d), a).start()

    def send_rows():
        c_load.wait()
        i_load.wait()
        shape = (A * CAP, rows)
        slot = lax.broadcasted_iota(jnp.int32, shape, 0)
        row = lax.broadcasted_iota(jnp.int32, shape, 1)
        one = lax.broadcasted_iota(jnp.int32, (rows, rows), 0)
        two = lax.broadcasted_iota(jnp.int32, (rows, rows), 1)
        earlier = as_bits((one // RD == two // RD) & (one < two))
        theirs = i_buf[...] == slot // CAP
        rank = dot(as_bits(theirs), earlier)
        chosen = as_bits(theirs & (rank == (slot % CAP).astype(jnp.float32)))
        local = as_bits(
            (lax.broadcasted_iota(jnp.int32, (rows, RP), 0) - a * RD
             == lax.broadcasted_iota(jnp.int32, (rows, RP), 1))
            & (lax.broadcasted_iota(jnp.int32, (rows, RP), 1) < RD)
        )
        chosen = dot(chosen, local).astype(jnp.bfloat16)
        p_buf[...] = jnp.zeros((RP, width), jnp.bfloat16)
        p_buf[pl.ds(0, RD), :] = r_buf[...]
        packed = dot(chosen, p_buf[...])
        for j in range(A):
            o_buf[j] = packed[j * CAP : (j + 1) * CAP].astype(jnp.bfloat16)
        for d in range(1, A):
            c_copy(back_peer(d), a).start()
        c_buf[a] = o_buf[a]
        own = i_buf[...] == a
        own = own & (row >= 0)
        rank = dot(as_bits(own), earlier)
        mine = own & (row // RD == slot // CAP) & (rank == (slot % CAP).astype(jnp.float32))
        pick_buf[...] = as_bits(mine)

    def project_rows():
        u_load.wait()
        remote(c_others, c_others, cs_sem, cr_sem, s, a).wait_recv()
        for j in range(A):
            q_buf[j * CAP : (j + 1) * CAP, :] = c_buf[j].astype(jnp.float32)
        back = dot_t(u_buf[...], q_buf[...].astype(jnp.bfloat16)).astype(jnp.bfloat16)
        back_buf[...] = dot(back, pick_buf[...])

    @pl.when(s >= 2)
    def _():
        send_rows()

    remote(g_others, g_others, gs_sem, gr_sem, s, a).wait_recv()

    @pl.when(s >= 2)
    def _():
        project_rows()

    d_load.wait()
    pltpu.make_async_copy(w_ref.at[0], w_buf, w_sem).wait()

    def micro(m, carry):
        start = pl.multiple_of(m * MR, MR)
        squares = jnp.zeros((MR, 128), jnp.float32)
        for d in range(A):
            j = peer(d)
            if d == 0:

                @pl.when(s > 0)
                def _():
                    h_copy(m, a, a).wait_recv()

            else:
                h_copy(m, a, j).wait_recv()
            h = h_buf[m, j].astype(jnp.float32)
            for t in range(C // 128):
                part = h[:, t * 128 : (t + 1) * 128]
                squares = squares + part * part
            h = h * g_buf[j]
            scaled = h.astype(jnp.bfloat16)
            n_buf[j, pl.ds(start, MR), :] = h
            part = dot(scaled, w_buf[pl.ds(pl.multiple_of(j * C, C), C), :])
            if d == 0:
                acc_buf[...] = part
            elif d < A - 1:
                acc_buf[...] += part
        inverse = lax.rsqrt(jnp.sum(squares, axis=1, keepdims=True) / width + epsilon)
        total = acc_buf[...] + part
        result = (h_buf[m, a].astype(jnp.float32) + total * inverse).astype(jnp.bfloat16)
        s_buf[m] = result

        @pl.when(s < S - 1)
        def _():
            for d in order:
                h_copy(m, back_peer(d), a).start()

        hid_ref[0, pl.ds(start, MR), :] = result
        inv_buf[pl.ds(start, MR), :] = jnp.broadcast_to(inverse, (MR, 128))
        return carry

    lax.fori_loop(0, NM, micro, 0)

    def release(section):
        pl.semaphore_signal(go_sem, inc=1, device_id=(section, a), device_id_type=MESH)

    @pl.when(s == 2)
    def _():
        release(1)

    @pl.when(s == 1)
    def _():
        pl.semaphore_wait(go_sem, 1)
        release(0)

    @pl.when(s == 0)
    def _():
        pl.semaphore_wait(go_sem, 1)

    @pl.when(s < 2)
    def _():
        send_rows()
        project_rows()

    eye = (lax.broadcasted_iota(jnp.int32, (rows, rows), 0)
           == lax.broadcasted_iota(jnp.int32, (rows, rows), 1))
    inverse = jnp.sum(jnp.where(eye, inv_buf[:, :1], 0.0), axis=0, keepdims=True)
    back = (back_buf[...] * inverse).astype(jnp.bfloat16)
    low = jnp.zeros(back.shape, jnp.float32)
    for j in range(A):
        block = n_buf[j].astype(jnp.bfloat16)
        low = low + dot_t(d_buf[:, j * C : (j + 1) * C], block)
        dgrad_ref[0, 0, :, j * C : (j + 1) * C] = adapter_scale * dot(back, block)
    low = (low * inverse).astype(jnp.bfloat16)
    low_mine = dot_t(low, pick_buf[...]).astype(jnp.bfloat16)
    ugrad_ref[0, 0] = adapter_scale * dot(low_mine, q_buf[...].astype(jnp.bfloat16))

    remote(g_others, g_others, gs_sem, gr_sem, s, a).wait_send()
    remote(c_others, c_others, cs_sem, cr_sem, s, a).wait_send()

    @pl.when(s == 0)
    def _():
        sent = h_buf.at[0, pl.ds(0, A - 1)]
        remote(sent, sent, xs_sem, xs_sem, s, a).wait_send()

    @pl.when(s == donor)
    def _():
        sent = h_buf.at[pl.ds(0, NM - 1), pl.ds(0, A - 1)]
        remote(sent, sent, xs_sem, xs_sem, s, a).wait_send()

    @pl.when(s < S - 1)
    def _():
        remote(h_buf, h_buf, hs_sem, hs_sem, s, a).wait_send()


def store(*refs):
    copies = [
        pltpu.make_async_copy(refs[k], refs[3 + k], refs[6].at[k]) for k in range(3)
    ]
    for copy in copies:
        copy.start()
    for copy in copies:
        copy.wait()


def store(*refs):
    copies = [
        pltpu.make_async_copy(refs[k], refs[3 + k], refs[6].at[k]) for k in range(3)
    ]
    for copy in copies:
        copy.start()
    for copy in copies:
        copy.wait()


def body(S, A, x, gains, frozen, down, up, idx, cot):
    rows, C = x.shape
    width = C * A
    rank = down.shape[2]
    MR = MICRO_ROWS
    NM = rows // MR
    RP = -(-cot.shape[1] // 16) * 16
    args = (x, gains, frozen, down, up, idx.T, cot)
    vmem = pl.BlockSpec(memory_space=pltpu.VMEM)
    hbm = pl.BlockSpec(memory_space=pltpu.HBM)
    dma = pltpu.SemaphoreType.DMA
    shapes = (
        jax.ShapeDtypeStruct((1, rows, C), jnp.bfloat16),
        jax.ShapeDtypeStruct((1, 1, rank, width), jnp.float32),
        jax.ShapeDtypeStruct((1, 1, rank, width), jnp.float32),
    )
    results = pl.pallas_call(
        functools.partial(relay, S, A),
        out_shape=shapes,
        in_specs=[hbm] * 7,
        out_specs=(vmem, vmem, vmem),
        scratch_shapes=[
            pltpu.VMEM((width, C), jnp.bfloat16),
            pltpu.VMEM((NM, A, MR, C), jnp.bfloat16),
            pltpu.VMEM((NM, MR, C), jnp.bfloat16),
            pltpu.VMEM((NM, MR, C), jnp.bfloat16),
            pltpu.VMEM((A, 1, C), jnp.float32),
            pltpu.VMEM((A, rows, C), jnp.float32),
            pltpu.VMEM((rows, 128), jnp.float32),
            pltpu.VMEM((A, CAP, width), jnp.bfloat16),
            pltpu.VMEM((MR, C), jnp.float32),
            pltpu.VMEM((rank, width), jnp.bfloat16),
            pltpu.VMEM((rank, width), jnp.bfloat16),
            pltpu.VMEM((1, rows), jnp.int32),
            pltpu.VMEM((cot.shape[1], width), jnp.bfloat16),
            pltpu.VMEM((rank, rows), jnp.float32),
            pltpu.VMEM((A * CAP, rows), jnp.bfloat16),
            pltpu.VMEM((RP, width), jnp.bfloat16),
            pltpu.VMEM((A, CAP, width), jnp.bfloat16),
            pltpu.VMEM((A * CAP, width), jnp.float32),
            pltpu.SemaphoreType.REGULAR,
            dma((5,)),
            dma,
            dma,
            dma,
            dma,
            dma((NM, A)),
            dma,
            dma,
            dma,
            dma,
        ],
        compiler_params=pltpu.CompilerParams(
            collective_id=0, has_side_effects=True, vmem_limit_bytes=48 * 1024 * 1024
        ),
        name="relay",
    )(*[pltpu.with_memory_space_constraint(v, pltpu.HBM) for v in args])
    return pl.pallas_call(
        store,
        out_shape=shapes,
        in_specs=[vmem] * 3,
        out_specs=(hbm, hbm, hbm),
        scratch_shapes=[dma((3,))],
        name="store",
    )(*[pltpu.with_memory_space_constraint(v, pltpu.VMEM) for v in results])


def solution(mesh):
    in_specs = (
        P(None, "adapter"),
        P("section", "adapter"),
        P("section", None, "adapter"),
        P("section", "adapter", None, None),
        P("section", "adapter", None, None),
        P(),
        P("section", "adapter", None),
    )
    out_specs = (
        P("section", None, "adapter"),
        P("section", "adapter", None, None),
        P("section", "adapter", None, None),
    )
    step = functools.partial(body, mesh.shape["section"], mesh.shape["adapter"])
    return jax.shard_map(step, mesh=mesh, in_specs=in_specs, out_specs=out_specs, check_vma=False)
```

```python
import functools
import jax
import jax.numpy as jnp
from jax import lax
from jax.experimental import pallas as pl
from jax.experimental.pallas import tpu as pltpu
from jax.sharding import PartitionSpec as P

MICRO_ROWS = 8
DONOR = 3
CAP = 4
epsilon = 1e-05
adapter_scale = 2.0
MESH = pl.DeviceIdType.MESH
CONTRACT_LAST = (((1,), (1,)), ((), ()))


def as_bits(mask):
    return jnp.where(mask, 1.0, 0.0).astype(jnp.bfloat16)


def dot(a, b):
    return jnp.dot(a, b, preferred_element_type=jnp.float32)


def dot_t(a, b):
    return lax.dot_general(a, b, CONTRACT_LAST, preferred_element_type=jnp.float32)


def relay(
    S,
    A,
    x_ref,
    gain_ref,
    w_ref,
    down_ref,
    up_ref,
    idx_ref,
    cot_ref,
    hid_ref,
    n_buf,
    inv_buf,
    d_buf,
    back_buf,
    pick_buf,
    q_buf,
    w_buf,
    h_buf,
    x_buf,
    s_buf,
    g_buf,
    c_buf,
    acc_buf,
    u_buf,
    i_buf,
    r_buf,
    p_buf,
    o_buf,
    go_sem,
    in_sem,
    x_sem,
    w_sem,
    xs_sem,
    hs_sem,
    hr_sem,
    gs_sem,
    gr_sem,
    cs_sem,
    cr_sem,
):
    s = lax.axis_index("section")
    a = lax.axis_index("adapter")
    NM, _, MR, C = h_buf.shape
    rows = n_buf.shape[1]
    width = A * C
    RD = cot_ref.shape[1]
    RP = p_buf.shape[0]
    paired = A & (A - 1) == 0
    order = [0, *range(A // 2, A), *range(1, A // 2)]
    donor = DONOR

    def w_copy(j):
        part = pl.ds(pl.multiple_of(j * C, C), C)
        return pltpu.make_async_copy(w_ref.at[0, part], w_buf.at[part], w_sem)

    def peer(d):
        if not paired:
            return lax.rem(a + d, A)
        place, bit = 0, 1
        while bit < A:
            place = place + lax.rem(a // bit + (d // bit) % 2, 2) * bit
            bit *= 2
        return place

    def back_peer(d):
        return peer(d) if paired else lax.rem(a + A - d, A)

    barrier = pltpu.get_barrier_semaphore()

    def greet(section, j):
        pl.semaphore_signal(
            barrier, inc=1, device_id=(section, j), device_id_type=MESH
        )

    for d in range(A - 1, 0, -1):
        greet(s, peer(d))

    @pl.when(s > 0)
    def _():
        for d in range(A - 1, -1, -1):
            greet(s - 1, peer(d))

    @pl.when(s < S - 1)
    def _():
        for d in range(A - 1, -1, -1):
            greet(s + 1, peer(d))

    @pl.when(s == 0)
    def _():
        for d in range(A - 1, 0, -1):
            greet(donor, peer(d))

    g_load = pltpu.make_async_copy(gain_ref, g_buf.at[a], in_sem.at[0])
    c_load = pltpu.make_async_copy(cot_ref.at[0], r_buf, in_sem.at[1])
    d_load = pltpu.make_async_copy(down_ref.at[0, 0], d_buf, in_sem.at[2])
    u_load = pltpu.make_async_copy(up_ref.at[0, 0], u_buf, in_sem.at[3])
    i_load = pltpu.make_async_copy(idx_ref, i_buf, in_sem.at[4])

    def x_load(m):
        return pltpu.make_async_copy(
            x_ref.at[pl.ds(m * MR, MR)], h_buf.at[m, a], x_sem
        )

    g_load.start()

    @pl.when(s == 0)
    def _():
        for m in range(NM):
            x_load(m).start()

    def x_fetch(m):
        return pltpu.make_async_copy(
            x_ref.at[pl.ds(m * MR, MR)], x_buf.at[m], x_sem
        )

    @pl.when(s == donor)
    def _():
        for m in range(1, NM):
            x_fetch(m).start()

    for d in range(A):
        w_copy(peer(d)).start()
    for load in (c_load, d_load, u_load, i_load):
        load.start()

    def remote(src, dst, send, recv, section, j):
        return pltpu.make_async_remote_copy(
            src_ref=src,
            dst_ref=dst,
            send_sem=send,
            recv_sem=recv,
            device_id=(section, j),
            device_id_type=MESH,
        )

    def x_copy(m, j, block):
        return remote(
            h_buf.at[m, a],
            h_buf.at[m, block],
            xs_sem,
            hr_sem.at[m, block],
            s,
            j,
        )

    def y_copy(m, j, block):
        return remote(
            x_buf.at[m],
            h_buf.at[m, block],
            xs_sem,
            hr_sem.at[m, block],
            0,
            j,
        )

    def h_copy(m, j, block):
        return remote(
            s_buf.at[m], h_buf.at[m, block], hs_sem, hr_sem.at[m, block], s + 1, j
        )

    def g_copy(j, block):
        return remote(g_buf.at[a], g_buf.at[block], gs_sem, gr_sem, s, j)

    def c_copy(j, block):
        return remote(o_buf.at[j], c_buf.at[block], cs_sem, cr_sem, s, j)

    g_others = g_buf.at[pl.ds(0, A - 1)]
    c_others = c_buf.at[pl.ds(0, A - 1)]
    g_load.wait()

    @pl.when(s == 0)
    def _():
        pltpu.make_async_copy(x_buf, h_buf.at[:, a], x_sem).wait()

    before = (s + S - 1) // S
    after = (2 * S - 2 - s) // S
    count = A - 1 + A * (before + after)
    pl.semaphore_wait(barrier, count + jnp.where(s == donor, A - 1, 0))

    @pl.when(s == 0)
    def _():
        for d in range(A - 1, 0, -1):
            x_copy(0, back_peer(d), a).start()
            g_copy(back_peer(d), a).start()

    @pl.when(s == donor)
    def _():
        late = x_buf.at[pl.ds(1, NM - 1)]
        pltpu.make_async_copy(late, late, x_sem).wait()
        for m in range(1, NM):
            for d in range(A - 1, 0, -1):
                y_copy(m, back_peer(d), a).start()

    @pl.when(s > 0)
    def _():
        for d in range(A - 1, 0, -1):
            g_copy(back_peer(d), a).start()

    def send_rows():
        c_load.wait()
        i_load.wait()
        shape = (A * CAP, rows)
        slot = lax.broadcasted_iota(jnp.int32, shape, 0)
        row = lax.broadcasted_iota(jnp.int32, shape, 1)
        one = lax.broadcasted_iota(jnp.int32, (rows, rows), 0)
        two = lax.broadcasted_iota(jnp.int32, (rows, rows), 1)
        earlier = as_bits((one // RD == two // RD) & (one < two))
        theirs = i_buf[...] == slot // CAP
        rank = dot(as_bits(theirs), earlier)
        chosen = as_bits(theirs & (rank == (slot % CAP).astype(jnp.float32)))
        local = as_bits(
            (lax.broadcasted_iota(jnp.int32, (rows, RP), 0) - a * RD
             == lax.broadcasted_iota(jnp.int32, (rows, RP), 1))
            & (lax.broadcasted_iota(jnp.int32, (rows, RP), 1) < RD)
        )
        chosen = dot(chosen, local).astype(jnp.bfloat16)
        p_buf[...] = jnp.zeros((RP, width), jnp.bfloat16)
        p_buf[pl.ds(0, RD), :] = r_buf[...]
        packed = dot(chosen, p_buf[...])
        for j in range(A):
            o_buf[j] = packed[j * CAP : (j + 1) * CAP].astype(jnp.bfloat16)
        for d in range(1, A):
            c_copy(back_peer(d), a).start()
        c_buf[a] = o_buf[a]
        own = i_buf[...] == a
        own = own & (row >= 0)
        rank = dot(as_bits(own), earlier)
        mine = own & (row // RD == slot // CAP) & (rank == (slot % CAP).astype(jnp.float32))
        pick_buf[...] = as_bits(mine)

    def project_rows():
        u_load.wait()
        remote(c_others, c_others, cs_sem, cr_sem, s, a).wait_recv()
        for j in range(A):
            q_buf[j * CAP : (j + 1) * CAP, :] = c_buf[j].astype(jnp.float32)
        back = dot_t(u_buf[...], q_buf[...].astype(jnp.bfloat16)).astype(jnp.bfloat16)
        back_buf[...] = dot(back, pick_buf[...])

    @pl.when(s >= 2)
    def _():
        send_rows()

    remote(g_others, g_others, gs_sem, gr_sem, s, a).wait_recv()

    @pl.when(s >= 2)
    def _():
        project_rows()

    d_load.wait()
    pltpu.make_async_copy(w_ref.at[0], w_buf, w_sem).wait()

    def micro(m, carry):
        start = pl.multiple_of(m * MR, MR)
        squares = jnp.zeros((MR, 128), jnp.float32)
        for d in range(A):
            j = peer(d)
            if d == 0:

                @pl.when(s > 0)
                def _():
                    h_copy(m, a, a).wait_recv()

            else:
                h_copy(m, a, j).wait_recv()
            h = h_buf[m, j].astype(jnp.float32)
            for t in range(C // 128):
                part = h[:, t * 128 : (t + 1) * 128]
                squares = squares + part * part
            h = h * g_buf[j]
            scaled = h.astype(jnp.bfloat16)
            n_buf[j, pl.ds(start, MR), :] = h
            part = dot(scaled, w_buf[pl.ds(pl.multiple_of(j * C, C), C), :])
            if d == 0:
                acc_buf[...] = part
            elif d < A - 1:
                acc_buf[...] += part
        inverse = lax.rsqrt(jnp.sum(squares, axis=1, keepdims=True) / width + epsilon)
        total = acc_buf[...] + part
        result = (h_buf[m, a].astype(jnp.float32) + total * inverse).astype(jnp.bfloat16)
        s_buf[m] = result

        @pl.when(s < S - 1)
        def _():
            for d in order:
                h_copy(m, back_peer(d), a).start()

        hid_ref[0, pl.ds(start, MR), :] = result
        inv_buf[pl.ds(start, MR), :] = jnp.broadcast_to(inverse, (MR, 128))
        return carry

    lax.fori_loop(0, NM, micro, 0)

    def release(section):
        pl.semaphore_signal(go_sem, inc=1, device_id=(section, a), device_id_type=MESH)

    @pl.when(s == 2)
    def _():
        release(1)

    @pl.when(s == 1)
    def _():
        pl.semaphore_wait(go_sem, 1)
        release(0)

    @pl.when(s == 0)
    def _():
        pl.semaphore_wait(go_sem, 1)

    @pl.when(s < 2)
    def _():
        send_rows()
        project_rows()

    remote(g_others, g_others, gs_sem, gr_sem, s, a).wait_send()
    remote(c_others, c_others, cs_sem, cr_sem, s, a).wait_send()

    @pl.when(s == 0)
    def _():
        sent = h_buf.at[0, pl.ds(0, A - 1)]
        remote(sent, sent, xs_sem, xs_sem, s, a).wait_send()

    @pl.when(s == donor)
    def _():
        sent = h_buf.at[pl.ds(0, NM - 1), pl.ds(0, A - 1)]
        remote(sent, sent, xs_sem, xs_sem, s, a).wait_send()

    @pl.when(s < S - 1)
    def _():
        remote(h_buf, h_buf, hs_sem, hs_sem, s, a).wait_send()


def finish(
    hid,
    n,
    inv,
    down,
    back,
    pick,
    q,
    hid_out,
    dgrad_out,
    ugrad_out,
    dgrad,
    ugrad,
    sem,
):
    A, rows, C = n.shape
    hid_copy = pltpu.make_async_copy(hid, hid_out, sem.at[0])
    hid_copy.start()
    eye = (lax.broadcasted_iota(jnp.int32, (rows, rows), 0)
           == lax.broadcasted_iota(jnp.int32, (rows, rows), 1))
    inverse = jnp.sum(jnp.where(eye, inv[:, :1], 0.0), axis=0, keepdims=True)
    scaled = (back[...] * inverse).astype(jnp.bfloat16)
    low = jnp.zeros(back.shape, jnp.float32)
    for j in range(A):
        part = pl.ds(j * C, C)
        block = n[j].astype(jnp.bfloat16)
        low = low + dot_t(down[:, part], block)
        dgrad[:, part] = adapter_scale * dot(scaled, block)
        pltpu.make_async_copy(
            dgrad.at[:, part], dgrad_out.at[0, 0, :, part], sem.at[1]
        ).start()
    low = (low * inverse).astype(jnp.bfloat16)
    low_mine = dot_t(low, pick[...]).astype(jnp.bfloat16)
    for j in range(A):
        part = pl.ds(j * C, C)
        ugrad[:, part] = adapter_scale * dot(low_mine, q[:, part].astype(jnp.bfloat16))
        pltpu.make_async_copy(
            ugrad.at[:, part], ugrad_out.at[0, 0, :, part], sem.at[2]
        ).start()
    hid_copy.wait()
    pltpu.make_async_copy(dgrad, dgrad_out.at[0, 0], sem.at[1]).wait()
    pltpu.make_async_copy(ugrad, ugrad_out.at[0, 0], sem.at[2]).wait()


def body(S, A, x, gains, frozen, down, up, idx, cot):
    rows, C = x.shape
    width = C * A
    rank = down.shape[2]
    MR = MICRO_ROWS
    NM = rows // MR
    RP = -(-cot.shape[1] // 16) * 16
    args = (x, gains, frozen, down, up, idx.T, cot)
    vmem = pl.BlockSpec(memory_space=pltpu.VMEM)
    hbm = pl.BlockSpec(memory_space=pltpu.HBM)
    dma = pltpu.SemaphoreType.DMA
    shapes = (
        jax.ShapeDtypeStruct((1, rows, C), jnp.bfloat16),
        jax.ShapeDtypeStruct((1, 1, rank, width), jnp.float32),
        jax.ShapeDtypeStruct((1, 1, rank, width), jnp.float32),
    )
    results = pl.pallas_call(
        functools.partial(relay, S, A),
        out_shape=(
            shapes[0],
            jax.ShapeDtypeStruct((A, rows, C), jnp.float32),
            jax.ShapeDtypeStruct((rows, 128), jnp.float32),
            jax.ShapeDtypeStruct((rank, width), jnp.bfloat16),
            jax.ShapeDtypeStruct((rank, rows), jnp.float32),
            jax.ShapeDtypeStruct((A * CAP, rows), jnp.bfloat16),
            jax.ShapeDtypeStruct((A * CAP, width), jnp.float32),
        ),
        in_specs=[hbm] * 7,
        out_specs=(vmem,) * 7,
        scratch_shapes=[
            pltpu.VMEM((width, C), jnp.bfloat16),
            pltpu.VMEM((NM, A, MR, C), jnp.bfloat16),
            pltpu.VMEM((NM, MR, C), jnp.bfloat16),
            pltpu.VMEM((NM, MR, C), jnp.bfloat16),
            pltpu.VMEM((A, 1, C), jnp.float32),
            pltpu.VMEM((A, CAP, width), jnp.bfloat16),
            pltpu.VMEM((MR, C), jnp.float32),
            pltpu.VMEM((rank, width), jnp.bfloat16),
            pltpu.VMEM((1, rows), jnp.int32),
            pltpu.VMEM((cot.shape[1], width), jnp.bfloat16),
            pltpu.VMEM((RP, width), jnp.bfloat16),
            pltpu.VMEM((A, CAP, width), jnp.bfloat16),
            pltpu.SemaphoreType.REGULAR,
            dma((5,)),
            dma,
            dma,
            dma,
            dma,
            dma((NM, A)),
            dma,
            dma,
            dma,
            dma,
        ],
        compiler_params=pltpu.CompilerParams(
            collective_id=0, has_side_effects=True, vmem_limit_bytes=48 * 1024 * 1024
        ),
        name="relay",
    )(*[pltpu.with_memory_space_constraint(v, pltpu.HBM) for v in args])
    return pl.pallas_call(
        finish,
        out_shape=shapes,
        in_specs=[vmem] * 7,
        out_specs=(hbm, hbm, hbm),
        scratch_shapes=[
            pltpu.VMEM((rank, width), jnp.float32),
            pltpu.VMEM((rank, width), jnp.float32),
            dma((3,)),
        ],
        compiler_params=pltpu.CompilerParams(vmem_limit_bytes=16 * 1024 * 1024),
        name="finish",
    )(*[pltpu.with_memory_space_constraint(v, pltpu.VMEM) for v in results])


def solution(mesh):
    in_specs = (
        P(None, "adapter"),
        P("section", "adapter"),
        P("section", None, "adapter"),
        P("section", "adapter", None, None),
        P("section", "adapter", None, None),
        P(),
        P("section", "adapter", None),
    )
    out_specs = (
        P("section", None, "adapter"),
        P("section", "adapter", None, None),
        P("section", "adapter", None, None),
    )
    step = functools.partial(body, mesh.shape["section"], mesh.shape["adapter"])
    return jax.shard_map(step, mesh=mesh, in_specs=in_specs, out_specs=out_specs, check_vma=False)
```

```python
import functools
import jax
import jax.numpy as jnp
from jax import lax
from jax.experimental import pallas as pl
from jax.experimental.pallas import tpu as pltpu
from jax.sharding import PartitionSpec as P

MICRO_ROWS = 8
DONOR = 3
CAP = 4
epsilon = 1e-05
adapter_scale = 2.0
MESH = pl.DeviceIdType.MESH
CONTRACT_LAST = (((1,), (1,)), ((), ()))


def as_bits(mask):
    return jnp.where(mask, 1.0, 0.0).astype(jnp.bfloat16)


def dot(a, b):
    return jnp.dot(a, b, preferred_element_type=jnp.float32)


def dot_t(a, b):
    return lax.dot_general(a, b, CONTRACT_LAST, preferred_element_type=jnp.float32)


def relay(
    S,
    A,
    x_ref,
    gain_ref,
    w_ref,
    down_ref,
    up_ref,
    idx_ref,
    cot_ref,
    hid_ref,
    n_buf,
    inv_buf,
    d_buf,
    back_buf,
    pick_buf,
    q_buf,
    w_buf,
    h_buf,
    x_buf,
    s_buf,
    g_buf,
    c_buf,
    acc_buf,
    u_buf,
    i_buf,
    r_buf,
    p_buf,
    o_buf,
    go_sem,
    in_sem,
    x_sem,
    w_sem,
    xs_sem,
    hs_sem,
    hr_sem,
    gs_sem,
    gr_sem,
    cs_sem,
    cr_sem,
):
    s = lax.axis_index("section")
    a = lax.axis_index("adapter")
    NM, _, MR, C = h_buf.shape
    rows = n_buf.shape[1]
    width = A * C
    RD = cot_ref.shape[1]
    RP = p_buf.shape[0]
    paired = A & (A - 1) == 0
    order = [*range(A // 2, A), 0, *range(1, A // 2)]
    donor = DONOR

    def w_copy(j):
        part = pl.ds(pl.multiple_of(j * C, C), C)
        return pltpu.make_async_copy(w_ref.at[0, part], w_buf.at[part], w_sem)

    def peer(d):
        if not paired:
            return lax.rem(a + d, A)
        place, bit = 0, 1
        while bit < A:
            place = place + lax.rem(a // bit + (d // bit) % 2, 2) * bit
            bit *= 2
        return place

    def back_peer(d):
        return peer(d) if paired else lax.rem(a + A - d, A)

    barrier = pltpu.get_barrier_semaphore()

    def greet(section, j):
        pl.semaphore_signal(
            barrier, inc=1, device_id=(section, j), device_id_type=MESH
        )

    for d in range(A - 1, 0, -1):
        greet(s, peer(d))

    @pl.when(s > 0)
    def _():
        for d in range(A - 1, -1, -1):
            greet(s - 1, peer(d))

    @pl.when(s < S - 1)
    def _():
        for d in range(A - 1, -1, -1):
            greet(s + 1, peer(d))

    @pl.when(s == 0)
    def _():
        for d in range(A - 1, 0, -1):
            greet(donor, peer(d))

    g_load = pltpu.make_async_copy(gain_ref, g_buf.at[a], in_sem.at[0])
    c_load = pltpu.make_async_copy(cot_ref.at[0], r_buf, in_sem.at[1])
    d_load = pltpu.make_async_copy(down_ref.at[0, 0], d_buf, in_sem.at[2])
    u_load = pltpu.make_async_copy(up_ref.at[0, 0], u_buf, in_sem.at[3])
    i_load = pltpu.make_async_copy(idx_ref, i_buf, in_sem.at[4])

    def x_load(m):
        return pltpu.make_async_copy(
            x_ref.at[pl.ds(m * MR, MR)], h_buf.at[m, a], x_sem
        )

    g_load.start()

    @pl.when(s == 0)
    def _():
        for m in range(NM):
            x_load(m).start()

    def x_fetch(m):
        return pltpu.make_async_copy(
            x_ref.at[pl.ds(m * MR, MR)], x_buf.at[m], x_sem
        )

    @pl.when(s == donor)
    def _():
        for m in range(1, NM):
            x_fetch(m).start()

    for d in range(A):
        w_copy(peer(d)).start()
    for load in (c_load, d_load, u_load, i_load):
        load.start()

    def remote(src, dst, send, recv, section, j):
        return pltpu.make_async_remote_copy(
            src_ref=src,
            dst_ref=dst,
            send_sem=send,
            recv_sem=recv,
            device_id=(section, j),
            device_id_type=MESH,
        )

    def x_copy(m, j, block):
        return remote(
            h_buf.at[m, a],
            h_buf.at[m, block],
            xs_sem,
            hr_sem.at[m, block],
            s,
            j,
        )

    def y_copy(m, j, block):
        return remote(
            x_buf.at[m],
            h_buf.at[m, block],
            xs_sem,
            hr_sem.at[m, block],
            0,
            j,
        )

    def h_copy(m, j, block):
        return remote(
            s_buf.at[m], h_buf.at[m, block], hs_sem, hr_sem.at[m, block], s + 1, j
        )

    def g_copy(j, block):
        return remote(g_buf.at[a], g_buf.at[block], gs_sem, gr_sem, s, j)

    def c_copy(j, block):
        return remote(o_buf.at[j], c_buf.at[block], cs_sem, cr_sem, s, j)

    g_others = g_buf.at[pl.ds(0, A - 1)]
    c_others = c_buf.at[pl.ds(0, A - 1)]
    g_load.wait()

    @pl.when(s == 0)
    def _():
        pltpu.make_async_copy(x_buf, h_buf.at[:, a], x_sem).wait()

    before = (s + S - 1) // S
    after = (2 * S - 2 - s) // S
    count = A - 1 + A * (before + after)
    pl.semaphore_wait(barrier, count + jnp.where(s == donor, A - 1, 0))

    @pl.when(s == 0)
    def _():
        for d in range(A - 1, 0, -1):
            x_copy(0, back_peer(d), a).start()
            g_copy(back_peer(d), a).start()

    @pl.when(s == donor)
    def _():
        late = x_buf.at[pl.ds(1, NM - 1)]
        pltpu.make_async_copy(late, late, x_sem).wait()
        for m in range(1, NM):
            for d in range(A - 1, 0, -1):
                y_copy(m, back_peer(d), a).start()

    @pl.when(s > 0)
    def _():
        for d in range(A - 1, 0, -1):
            g_copy(back_peer(d), a).start()

    def send_rows():
        c_load.wait()
        i_load.wait()
        shape = (A * CAP, rows)
        slot = lax.broadcasted_iota(jnp.int32, shape, 0)
        row = lax.broadcasted_iota(jnp.int32, shape, 1)
        one = lax.broadcasted_iota(jnp.int32, (rows, rows), 0)
        two = lax.broadcasted_iota(jnp.int32, (rows, rows), 1)
        earlier = as_bits((one // RD == two // RD) & (one < two))
        theirs = i_buf[...] == slot // CAP
        rank = dot(as_bits(theirs), earlier)
        chosen = as_bits(theirs & (rank == (slot % CAP).astype(jnp.float32)))
        local = as_bits(
            (lax.broadcasted_iota(jnp.int32, (rows, RP), 0) - a * RD
             == lax.broadcasted_iota(jnp.int32, (rows, RP), 1))
            & (lax.broadcasted_iota(jnp.int32, (rows, RP), 1) < RD)
        )
        chosen = dot(chosen, local).astype(jnp.bfloat16)
        p_buf[...] = jnp.zeros((RP, width), jnp.bfloat16)
        p_buf[pl.ds(0, RD), :] = r_buf[...]
        packed = dot(chosen, p_buf[...])
        for j in range(A):
            o_buf[j] = packed[j * CAP : (j + 1) * CAP].astype(jnp.bfloat16)
        for d in range(1, A):
            c_copy(back_peer(d), a).start()
        c_buf[a] = o_buf[a]
        own = i_buf[...] == a
        own = own & (row >= 0)
        rank = dot(as_bits(own), earlier)
        mine = own & (row // RD == slot // CAP) & (rank == (slot % CAP).astype(jnp.float32))
        pick_buf[...] = as_bits(mine)

    def project_rows():
        u_load.wait()
        remote(c_others, c_others, cs_sem, cr_sem, s, a).wait_recv()
        for j in range(A):
            q_buf[j * CAP : (j + 1) * CAP, :] = c_buf[j].astype(jnp.float32)
        back = dot_t(u_buf[...], q_buf[...].astype(jnp.bfloat16)).astype(jnp.bfloat16)
        back_buf[...] = dot(back, pick_buf[...])

    @pl.when(s >= 2)
    def _():
        send_rows()

    remote(g_others, g_others, gs_sem, gr_sem, s, a).wait_recv()

    @pl.when(s >= 2)
    def _():
        project_rows()

    d_load.wait()
    pltpu.make_async_copy(w_ref.at[0], w_buf, w_sem).wait()

    def micro(m, carry):
        start = pl.multiple_of(m * MR, MR)
        squares = jnp.zeros((MR, 128), jnp.float32)
        for d in range(A):
            j = peer(d)
            if d == 0:

                @pl.when(s > 0)
                def _():
                    h_copy(m, a, a).wait_recv()

            else:
                h_copy(m, a, j).wait_recv()
            h = h_buf[m, j].astype(jnp.float32)
            for t in range(C // 128):
                part = h[:, t * 128 : (t + 1) * 128]
                squares = squares + part * part
            h = h * g_buf[j]
            scaled = h.astype(jnp.bfloat16)
            n_buf[j, pl.ds(start, MR), :] = h
            part = dot(scaled, w_buf[pl.ds(pl.multiple_of(j * C, C), C), :])
            if d == 0:
                acc_buf[...] = part
            elif d < A - 1:
                acc_buf[...] += part
        inverse = lax.rsqrt(jnp.sum(squares, axis=1, keepdims=True) / width + epsilon)
        total = acc_buf[...] + part
        result = (h_buf[m, a].astype(jnp.float32) + total * inverse).astype(jnp.bfloat16)
        s_buf[m] = result

        @pl.when(s < S - 1)
        def _():
            for d in order:
                h_copy(m, back_peer(d), a).start()

        hid_ref[0, pl.ds(start, MR), :] = result
        inv_buf[pl.ds(start, MR), :] = jnp.broadcast_to(inverse, (MR, 128))
        return carry

    lax.fori_loop(0, NM, micro, 0)

    def release(section):
        pl.semaphore_signal(go_sem, inc=1, device_id=(section, a), device_id_type=MESH)

    @pl.when(s == 2)
    def _():
        release(1)

    @pl.when(s == 1)
    def _():
        pl.semaphore_wait(go_sem, 1)
        release(0)

    @pl.when(s == 0)
    def _():
        pl.semaphore_wait(go_sem, 1)

    @pl.when(s < 2)
    def _():
        send_rows()
        project_rows()

    remote(g_others, g_others, gs_sem, gr_sem, s, a).wait_send()
    remote(c_others, c_others, cs_sem, cr_sem, s, a).wait_send()

    @pl.when(s == 0)
    def _():
        sent = h_buf.at[0, pl.ds(0, A - 1)]
        remote(sent, sent, xs_sem, xs_sem, s, a).wait_send()

    @pl.when(s == donor)
    def _():
        sent = h_buf.at[pl.ds(0, NM - 1), pl.ds(0, A - 1)]
        remote(sent, sent, xs_sem, xs_sem, s, a).wait_send()

    @pl.when(s < S - 1)
    def _():
        remote(h_buf, h_buf, hs_sem, hs_sem, s, a).wait_send()


def finish(
    hid,
    n,
    inv,
    down,
    back,
    pick,
    q,
    hid_out,
    dgrad_out,
    ugrad_out,
    dgrad,
    ugrad,
    sem,
):
    A, rows, C = n.shape
    hid_copy = pltpu.make_async_copy(hid, hid_out, sem.at[0])
    hid_copy.start()
    eye = (lax.broadcasted_iota(jnp.int32, (rows, rows), 0)
           == lax.broadcasted_iota(jnp.int32, (rows, rows), 1))
    inverse = jnp.sum(jnp.where(eye, inv[:, :1], 0.0), axis=0, keepdims=True)
    scaled = (back[...] * inverse).astype(jnp.bfloat16)
    low = jnp.zeros(back.shape, jnp.float32)
    blocks = []
    for j in range(A):
        blocks.append(n[j].astype(jnp.bfloat16))
        low = low + dot_t(down[:, pl.ds(j * C, C)], blocks[j])
    for j in range(A):
        part = pl.ds(j * C, C)
        dgrad[:, part] = adapter_scale * dot(scaled, blocks[j])
    low = (low * inverse).astype(jnp.bfloat16)
    low_mine = dot_t(low, pick[...]).astype(jnp.bfloat16)
    pltpu.make_async_copy(dgrad, dgrad_out.at[0, 0], sem.at[1]).start()
    for k in range(2):
        part = pl.ds(k * (A * C // 2), A * C // 2)
        ugrad[:, part] = adapter_scale * dot(low_mine, q[:, part].astype(jnp.bfloat16))
        pltpu.make_async_copy(
            ugrad.at[:, part], ugrad_out.at[0, 0, :, part], sem.at[2]
        ).start()
    hid_copy.wait()
    pltpu.make_async_copy(dgrad, dgrad_out.at[0, 0], sem.at[1]).wait()
    pltpu.make_async_copy(ugrad, ugrad_out.at[0, 0], sem.at[2]).wait()


def body(S, A, x, gains, frozen, down, up, idx, cot):
    rows, C = x.shape
    width = C * A
    rank = down.shape[2]
    MR = MICRO_ROWS
    NM = rows // MR
    RP = -(-cot.shape[1] // 16) * 16
    args = (x, gains, frozen, down, up, idx.T, cot)
    vmem = pl.BlockSpec(memory_space=pltpu.VMEM)
    hbm = pl.BlockSpec(memory_space=pltpu.HBM)
    dma = pltpu.SemaphoreType.DMA
    shapes = (
        jax.ShapeDtypeStruct((1, rows, C), jnp.bfloat16),
        jax.ShapeDtypeStruct((1, 1, rank, width), jnp.float32),
        jax.ShapeDtypeStruct((1, 1, rank, width), jnp.float32),
    )
    results = pl.pallas_call(
        functools.partial(relay, S, A),
        out_shape=(
            shapes[0],
            jax.ShapeDtypeStruct((A, rows, C), jnp.float32),
            jax.ShapeDtypeStruct((rows, 128), jnp.float32),
            jax.ShapeDtypeStruct((rank, width), jnp.bfloat16),
            jax.ShapeDtypeStruct((rank, rows), jnp.float32),
            jax.ShapeDtypeStruct((A * CAP, rows), jnp.bfloat16),
            jax.ShapeDtypeStruct((A * CAP, width), jnp.float32),
        ),
        in_specs=[hbm] * 7,
        out_specs=(vmem,) * 7,
        scratch_shapes=[
            pltpu.VMEM((width, C), jnp.bfloat16),
            pltpu.VMEM((NM, A, MR, C), jnp.bfloat16),
            pltpu.VMEM((NM, MR, C), jnp.bfloat16),
            pltpu.VMEM((NM, MR, C), jnp.bfloat16),
            pltpu.VMEM((A, 1, C), jnp.float32),
            pltpu.VMEM((A, CAP, width), jnp.bfloat16),
            pltpu.VMEM((MR, C), jnp.float32),
            pltpu.VMEM((rank, width), jnp.bfloat16),
            pltpu.VMEM((1, rows), jnp.int32),
            pltpu.VMEM((cot.shape[1], width), jnp.bfloat16),
            pltpu.VMEM((RP, width), jnp.bfloat16),
            pltpu.VMEM((A, CAP, width), jnp.bfloat16),
            pltpu.SemaphoreType.REGULAR,
            dma((5,)),
            dma,
            dma,
            dma,
            dma,
            dma((NM, A)),
            dma,
            dma,
            dma,
            dma,
        ],
        compiler_params=pltpu.CompilerParams(
            collective_id=0, has_side_effects=True, vmem_limit_bytes=48 * 1024 * 1024
        ),
        name="relay",
    )(*[pltpu.with_memory_space_constraint(v, pltpu.HBM) for v in args])
    return pl.pallas_call(
        finish,
        out_shape=shapes,
        in_specs=[vmem] * 7,
        out_specs=(hbm, hbm, hbm),
        scratch_shapes=[
            pltpu.VMEM((rank, width), jnp.float32),
            pltpu.VMEM((rank, width), jnp.float32),
            dma((3,)),
        ],
        compiler_params=pltpu.CompilerParams(vmem_limit_bytes=16 * 1024 * 1024),
        name="finish",
    )(*[pltpu.with_memory_space_constraint(v, pltpu.VMEM) for v in results])


def solution(mesh):
    in_specs = (
        P(None, "adapter"),
        P("section", "adapter"),
        P("section", None, "adapter"),
        P("section", "adapter", None, None),
        P("section", "adapter", None, None),
        P(),
        P("section", "adapter", None),
    )
    out_specs = (
        P("section", None, "adapter"),
        P("section", "adapter", None, None),
        P("section", "adapter", None, None),
    )
    step = functools.partial(body, mesh.shape["section"], mesh.shape["adapter"])
    return jax.shard_map(step, mesh=mesh, in_specs=in_specs, out_specs=out_specs, check_vma=False)
```
